128 devices in a mesh: pts: 16 (over z, y), freq: 8 (over x, core).
Axes of the slice: x: 4, y: 4, z: 4, core: 2. Of those that a mesh axis runs over, the one named last changes fastest.
Arguments:
- spectra: bfloat16 [128, 5, 4096, 128], P('freq', None, 'pts'), parts along dimension 0, may hold values from -200 to 200, as said below
- weights: float32 [4096], P('pts'), as said below
Outputs:
- mode_shapes: bfloat16 [128, 5, 4096, 128], P('freq', None, 'pts'), parts along dimension 0
The draws below stay inside these ranges and needn't reach their ends.
There are 8 independent parts, one for each index of `freq`. The reference program is written for one: setup_inputs(seed, part) draws one part's arguments, and reference() takes and returns one part's arrays. A program takes and returns all parts, laid end to end along the dimension named above; an argument that names none is the same for every part. Nothing has to cross between parts.
Inputs may be any that keep to these rules, and one draw needn't show every extreme that they name: `spectra`: each row (frequency, variable, point) and each block's column pair has its own scale; the complex columns are independent. `weights`: Positive; their sum is of order one.
All inputs are finite; a program needn't handle non-finite values.
Results may differ from the reference program's by a relative error of at most 0.0054.
Values sent between devices are 32-bit elements; how exact they have to be, the bound alone decides.
No kernel may reach another device: no remote copies, remote signals or barrier semaphores. Data moves between devices by JAX's collectives and lax.ppermute only.
A program may use at most 64 MiB of HBM per device.

```python
import math
import jax
import jax.numpy as jnp
from jax import lax

BLOCKS = 64
VARS = 5
COLS = 128
FREQ_DEV = 16
NS_STEPS = 10
POINTS = 4096


def draw_spectra(key, part):
    key = jax.random.fold_in(key, 11)
    key_base = jax.random.fold_in(key, 1)
    key_cols = jax.random.fold_in(key, 3)
    key_rows = jax.random.fold_in(key, 4)
    shape = (FREQ_DEV, VARS, POINTS, 2 * BLOCKS)
    base = jnp.clip(jax.random.normal(key_base, shape, jnp.float32), -5.0, 5.0)
    row_scale = jnp.exp(jax.random.uniform(key_rows, (FREQ_DEV, VARS, POINTS, 1), jnp.float32, math.log(0.5), math.log(2.0)))
    col_scale = jnp.exp(jax.random.uniform(key_cols, (FREQ_DEV, 1, 1, BLOCKS), jnp.float32, 0.0, math.log(10.0)))
    col_scale = jnp.concatenate([col_scale, col_scale], -1)
    return (base * col_scale * row_scale).astype(jnp.bfloat16)


def draw_weights(key, part):
    key = jax.random.fold_in(key, 23)
    position = jnp.arange(POINTS).astype(jnp.float32) / POINTS
    trend = jnp.exp(math.log(3.0) * position)
    rough = jnp.exp(jax.random.uniform(key, (POINTS,), jnp.float32, math.log(0.5), math.log(2.0)))
    return (trend * rough / POINTS).astype(jnp.float32)


def setup_inputs(seed: int = 0, part: int = 0) -> dict:
    keys = jax.random.split(jax.random.key(seed), 3)
    part_keys = jax.random.split(jax.random.fold_in(keys[2], part), 3)
    return {
        "spectra": draw_spectra(jax.random.fold_in(jax.random.fold_in(keys[2], part), 71), part),
        "weights": draw_weights(jax.random.fold_in(keys[2], 71), part),
    }


def fold_cross(products):
    half_cols = products.shape[-1] // 2
    top_left = products[:half_cols, :half_cols]
    top_right = products[:half_cols, half_cols:]
    bottom_left = products[half_cols:, :half_cols]
    bottom_right = products[half_cols:, half_cols:]
    real_part = top_left + bottom_right
    imag_part = top_right - bottom_left
    upper_row = jnp.concatenate([real_part, imag_part], 1)
    lower_row = jnp.concatenate([-imag_part, real_part], 1)
    return jnp.concatenate([upper_row, lower_row], 0)

def reference(spectra, weights):
    results = []
    root_weights = jnp.sqrt(weights)
    for freq_index in range(FREQ_DEV):
        block = spectra[freq_index]
        weighted = (root_weights[None, :, None] * block.astype(jnp.float32)).astype(jnp.bfloat16)
        flat_rows = weighted.reshape(VARS * POINTS, COLS)
        products = jnp.dot(flat_rows.T.astype(jnp.float32), flat_rows.astype(jnp.float32), preferred_element_type=jnp.float32)
        cross_gram = fold_cross(products)
        upper_factor = jnp.linalg.cholesky(cross_gram).T
        frob_norm = jnp.sqrt(jnp.sum(upper_factor * upper_factor))
        polar = upper_factor / frob_norm
        for sweep in range(NS_STEPS):
            inner_gram = jnp.dot(polar.T, polar, precision=lax.Precision.HIGHEST)
            polar = 1.5 * polar - 0.5 * jnp.dot(polar, inner_gram, precision=lax.Precision.HIGHEST)
        mapping = lax.linalg.triangular_solve(upper_factor, polar, left_side=True, lower=False).astype(jnp.bfloat16)
        source_rows = block.reshape(VARS * POINTS, COLS)
        shapes = jnp.dot(source_rows.astype(jnp.float32), mapping.astype(jnp.float32), preferred_element_type=jnp.float32).astype(jnp.bfloat16)
        results.append(shapes.reshape(VARS, POINTS, COLS))
    return jnp.stack(results, 0)
```

```python
import jax
import jax.numpy as jnp
from jax import lax
from jax.experimental import pallas as pl
from jax.experimental.pallas import tpu as pltpu
from jax.sharding import PartitionSpec as P

NS_STEPS = 10
HALF = 64
COLS = 2 * HALF


def places():
    rows = lax.broadcasted_iota(jnp.int32, (HALF, HALF), 0)
    cols = lax.broadcasted_iota(jnp.int32, (HALF, HALF), 1)
    return rows, cols


def pack(real_part, imag_part):
    rows, cols = places()
    square = jnp.where(rows >= cols, real_part, imag_part)
    return jnp.concatenate([square[: HALF // 2], square[HALF // 2 :]], 1)


def unpack(packed):
    rows, cols = places()
    square = jnp.concatenate([packed[:, :HALF], packed[:, HALF:]], 0)
    flipped = square.T
    real_part = jnp.where(rows >= cols, square, flipped)
    imag_part = jnp.where(rows < cols, square, jnp.where(rows > cols, -flipped, 0.0))
    return real_part, imag_part


def real_form(real_part, imag_part):
    upper_row = jnp.concatenate([real_part, imag_part], 1)
    lower_row = jnp.concatenate([-imag_part, real_part], 1)
    return jnp.concatenate([upper_row, lower_row], 0)


def gram_kernel(spectra_ref, weights_ref, packed_ref, root_ref):
    @pl.when(pl.program_id(0) == 0)
    def _():
        for part in range(weights_ref.shape[0]):
            row = jnp.sqrt(weights_ref[part : part + 1, :])
            root_ref[part * COLS : (part + 1) * COLS, :] = jnp.broadcast_to(row, (COLS, COLS)).T

    for spot in range(spectra_ref.shape[0]):
        weighted = (root_ref[...][None] * spectra_ref[spot].astype(jnp.float32)).astype(jnp.bfloat16)
        rows = weighted.reshape(-1, COLS)
        products = lax.dot_general(
            rows, rows, (((0,), (0,)), ((), ())), preferred_element_type=jnp.float32
        )
        real_part = products[:HALF, :HALF] + products[HALF:, HALF:]
        imag_part = products[:HALF, HALF:] - products[HALF:, :HALF]
        packed_ref[spot] = pack(real_part, imag_part)


def split(value):
    high = value.astype(jnp.bfloat16)
    low = (value - high.astype(jnp.float32)).astype(jnp.bfloat16)
    return high, low


def left_of(value):
    return jnp.concatenate(split(value), 1)


def right_of(value):
    row = jnp.concatenate(split(value), 1)
    return jnp.concatenate([row, row], 0)


def product(left, right):
    both = jnp.dot(left, right, preferred_element_type=jnp.float32)
    return both[:, :COLS] + both[:, COLS:]


def polar_kernel(parts_ref, packed_ref):
    gram = real_form(*unpack(jnp.sum(parts_ref[...], 0)))
    rows = lax.broadcasted_iota(jnp.int32, (COLS, COLS), 0)
    cols = lax.broadcasted_iota(jnp.int32, (COLS, COLS), 1)
    ident = (rows == cols).astype(jnp.float32)
    trace = jnp.sum(gram * ident)
    inner = gram / trace
    factor = 1.5 * ident - 0.5 * inner
    mapping = factor / jnp.sqrt(trace)
    for sweep in range(NS_STEPS - 1):
        right = right_of(factor)
        half = product(left_of(inner), right)
        inner = product(left_of(half), right)
        factor = 1.5 * ident - 0.5 * inner
        mapping = product(left_of(mapping), right_of(factor))
    packed = pack(mapping[:HALF, :HALF], mapping[:HALF, HALF:])
    packed_ref[...] = jnp.broadcast_to(packed[None], packed_ref.shape)


def apply_kernel(packed_ref, spectra_ref, shapes_ref):
    for spot in range(spectra_ref.shape[0]):
        mapping = real_form(*unpack(packed_ref[spot])).astype(jnp.bfloat16)
        rows = spectra_ref[spot].reshape(-1, COLS)
        shapes = jnp.dot(rows, mapping, preferred_element_type=jnp.float32)
        shapes_ref[spot] = shapes.astype(jnp.bfloat16).reshape(shapes_ref.shape[1:])


def local(spectra, weights):
    freq_count, var_count, point_count, col_count = spectra.shape
    step = 2
    block = pl.BlockSpec((step, var_count, point_count, col_count), lambda f: (f, 0, 0, 0))
    small = pl.BlockSpec((step, HALF // 2, COLS), lambda f: (f, 0, 0))
    packed_shape = jax.ShapeDtypeStruct((freq_count, HALF // 2, COLS), jnp.float32)
    packed = pl.pallas_call(
        gram_kernel,
        grid=(freq_count // step,),
        in_specs=[block, pl.BlockSpec((point_count // COLS, COLS), lambda f: (0, 0))],
        out_specs=small,
        out_shape=packed_shape,
        scratch_shapes=[pltpu.VMEM((point_count, COLS), jnp.float32)],
    )(spectra, weights.reshape(point_count // COLS, COLS))
    parts = lax.all_to_all(packed, "pts", 0, 0, tiled=True)
    own = pl.pallas_call(
        polar_kernel,
        in_specs=[pl.BlockSpec(memory_space=pltpu.VMEM)],
        out_specs=pl.BlockSpec(memory_space=pltpu.VMEM),
        out_shape=packed_shape,
    )(parts)
    mappings = lax.all_to_all(own, "pts", 0, 0, tiled=True)
    return pl.pallas_call(
        apply_kernel,
        grid=(freq_count // step,),
        in_specs=[small, block],
        out_specs=block,
        out_shape=jax.ShapeDtypeStruct(spectra.shape, jnp.bfloat16),
    )(mappings, spectra)


def solution(mesh):
    in_specs = (P("freq", None, "pts", None), P("pts"))
    out_specs = P("freq", None, "pts", None)
    return jax.shard_map(local, mesh=mesh, in_specs=in_specs, out_specs=out_specs, check_vma=False)
```

```python
import jax
import jax.numpy as jnp
from jax import lax
from jax.experimental import pallas as pl
from jax.experimental.pallas import tpu as pltpu
from jax.sharding import PartitionSpec as P

NS_STEPS = 10
HALF = 64
COLS = 2 * HALF


def places():
    rows = lax.broadcasted_iota(jnp.int32, (HALF, HALF), 0)
    cols = lax.broadcasted_iota(jnp.int32, (HALF, HALF), 1)
    return rows, cols


def pack(real_part, imag_part):
    rows, cols = places()
    square = jnp.where(rows >= cols, real_part, imag_part)
    return jnp.concatenate([square[: HALF // 2], square[HALF // 2 :]], 1)


def unpack(packed):
    rows, cols = places()
    square = jnp.concatenate([packed[:, :HALF], packed[:, HALF:]], 0)
    flipped = square.T
    real_part = jnp.where(rows >= cols, square, flipped)
    imag_part = jnp.where(rows < cols, square, jnp.where(rows > cols, -flipped, 0.0))
    return real_part, imag_part


def real_form(real_part, imag_part):
    upper_row = jnp.concatenate([real_part, imag_part], 1)
    lower_row = jnp.concatenate([-imag_part, real_part], 1)
    return jnp.concatenate([upper_row, lower_row], 0)


def gram_kernel(spectra_ref, weights_ref, packed_ref, held_ref, near_ref, root_ref, near_sem, sems):
    freq_count = spectra_ref.shape[0]
    step = freq_count // sems.shape[0]

    def load(spot):
        place = pl.ds(spot * step, step)
        return pltpu.make_async_copy(spectra_ref.at[place], held_ref.at[place], sems.at[spot])

    near = pltpu.make_async_copy(weights_ref, near_ref, near_sem)
    near.start()
    for spot in range(sems.shape[0]):
        load(spot).start()
    near.wait()
    for part in range(near_ref.shape[0]):
        row = jnp.sqrt(near_ref[part : part + 1, :])
        root_ref[part * COLS : (part + 1) * COLS, :] = jnp.broadcast_to(row, (COLS, COLS)).T

    @pl.loop(0, sems.shape[0])
    def _(spot):
        load(spot).wait()
        for inside in range(step):
            freq = spot * step + inside
            weighted = (root_ref[...][None] * held_ref[freq].astype(jnp.float32)).astype(jnp.bfloat16)
            rows = weighted.reshape(-1, COLS)
            products = lax.dot_general(
                rows, rows, (((0,), (0,)), ((), ())), preferred_element_type=jnp.float32
            )
            real_part = products[:HALF, :HALF] + products[HALF:, HALF:]
            imag_part = products[:HALF, HALF:] - products[HALF:, :HALF]
            packed_ref[freq] = pack(real_part, imag_part)


def split(value):
    high = value.astype(jnp.bfloat16)
    low = (value - high.astype(jnp.float32)).astype(jnp.bfloat16)
    return high, low


def left_of(value):
    return jnp.concatenate(split(value), 1)


def right_of(value):
    row = jnp.concatenate(split(value), 1)
    return jnp.concatenate([row, row], 0)


def product(left, right):
    both = jnp.dot(left, right, preferred_element_type=jnp.float32)
    return both[:, :COLS] + both[:, COLS:]


def polar_kernel(parts_ref, packed_ref):
    gram = real_form(*unpack(jnp.sum(parts_ref[...], 0)))
    rows = lax.broadcasted_iota(jnp.int32, (COLS, COLS), 0)
    cols = lax.broadcasted_iota(jnp.int32, (COLS, COLS), 1)
    ident = (rows == cols).astype(jnp.float32)
    trace = jnp.sum(gram * ident)
    inner = gram / trace
    factor = 1.5 * ident - 0.5 * inner
    mapping = factor / jnp.sqrt(trace)
    for sweep in range(NS_STEPS - 1):
        right = right_of(factor)
        half = product(left_of(inner), right)
        inner = product(left_of(half), right)
        factor = 1.5 * ident - 0.5 * inner
        mapping = product(left_of(mapping), right_of(factor))
    packed = pack(mapping[:HALF, :HALF], mapping[:HALF, HALF:])
    packed_ref[...] = jnp.broadcast_to(packed[None], packed_ref.shape)


def apply_kernel(packed_ref, spectra_ref, shapes_ref, staged_ref, sems):
    freq_count = spectra_ref.shape[0]
    step = freq_count // sems.shape[0]

    def save(spot):
        place = pl.ds(spot * step, step)
        return pltpu.make_async_copy(staged_ref.at[place], shapes_ref.at[place], sems.at[spot])

    @pl.loop(0, sems.shape[0])
    def _(spot):
        for inside in range(step):
            freq = spot * step + inside
            mapping = real_form(*unpack(packed_ref[freq])).astype(jnp.bfloat16)
            rows = spectra_ref[freq].reshape(-1, COLS)
            shapes = jnp.dot(rows, mapping, preferred_element_type=jnp.float32)
            staged_ref[freq] = shapes.astype(jnp.bfloat16).reshape(staged_ref.shape[1:])
        save(spot).start()

    for spot in range(sems.shape[0]):
        save(spot).wait()


LOADS = 2
SAVES = 2
MIB = 1 << 20


def local(spectra, weights):
    freq_count, var_count, point_count, col_count = spectra.shape
    hbm = pl.BlockSpec(memory_space=pltpu.HBM)
    vmem = pl.BlockSpec(memory_space=pltpu.VMEM)
    packed_shape = (freq_count, HALF // 2, COLS)
    packed, held = pl.pallas_call(
        gram_kernel,
        in_specs=[hbm, hbm],
        out_specs=[vmem, vmem],
        out_shape=[pltpu.VMEM(packed_shape, jnp.float32), pltpu.VMEM(spectra.shape, spectra.dtype)],
        scratch_shapes=[
            pltpu.VMEM((point_count // COLS, COLS), jnp.float32),
            pltpu.VMEM((point_count, COLS), jnp.float32),
            pltpu.SemaphoreType.DMA,
            pltpu.SemaphoreType.DMA((LOADS,)),
        ],
        compiler_params=pltpu.CompilerParams(vmem_limit_bytes=8 * MIB),
        name="gram",
    )(
        pltpu.with_memory_space_constraint(spectra, pltpu.HBM),
        pltpu.with_memory_space_constraint(weights.reshape(point_count // COLS, COLS), pltpu.HBM),
    )
    parts = lax.all_to_all(packed, "pts", 0, 0, tiled=True)
    own = pl.pallas_call(
        polar_kernel,
        in_specs=[vmem],
        out_specs=vmem,
        out_shape=pltpu.VMEM(packed_shape, jnp.float32),
        compiler_params=pltpu.CompilerParams(vmem_limit_bytes=8 * MIB),
        name="polar",
    )(pltpu.with_memory_space_constraint(parts, pltpu.VMEM))
    mappings = lax.all_to_all(own, "pts", 0, 0, tiled=True)
    return pl.pallas_call(
        apply_kernel,
        in_specs=[vmem, vmem],
        out_specs=hbm,
        out_shape=jax.ShapeDtypeStruct(spectra.shape, jnp.bfloat16),
        scratch_shapes=[
            pltpu.VMEM(spectra.shape, jnp.bfloat16),
            pltpu.SemaphoreType.DMA((SAVES,)),
        ],
        compiler_params=pltpu.CompilerParams(vmem_limit_bytes=16 * MIB),
        name="apply",
    )(pltpu.with_memory_space_constraint(mappings, pltpu.VMEM), held)


def solution(mesh):
    in_specs = (P("freq", None, "pts", None), P("pts"))
    out_specs = P("freq", None, "pts", None)
    return jax.shard_map(local, mesh=mesh, in_specs=in_specs, out_specs=out_specs, check_vma=False)
```

```python
import jax
import jax.numpy as jnp
from jax import lax
from jax.experimental import pallas as pl
from jax.experimental.pallas import tpu as pltpu
from jax.sharding import PartitionSpec as P

NS_STEPS = 10
HALF = 64
COLS = 2 * HALF


def places(rows):
    row = lax.broadcasted_iota(jnp.int32, (rows, COLS), 0)
    col = lax.broadcasted_iota(jnp.int32, (rows, COLS), 1)
    return row % HALF, col % HALF, row < HALF, col < HALF


def pack(square):
    row, col, _, left = places(HALF)
    top, bottom = square[:HALF], square[HALF:]
    lower = row >= col
    chosen = jnp.where(left == lower, top, jnp.where(left, -bottom, bottom))
    upper_rows, lower_rows = chosen[: HALF // 2], chosen[HALF // 2 :]
    left = left[: HALF // 2]
    keep = jnp.where(left, upper_rows, lower_rows)
    move = jnp.where(left, lower_rows, upper_rows)
    return keep + pltpu.roll(move, HALF, 1)


def unpack(packed):
    row, col, above, left = places(COLS)
    turned = pltpu.roll(packed, HALF, 1)
    half_left = left[: HALF // 2]
    upper_rows = jnp.where(half_left, packed, turned)
    lower_rows = jnp.where(half_left, turned, packed)
    tiled = jnp.concatenate([upper_rows, lower_rows, upper_rows, lower_rows], 0)
    flipped = tiled.T
    real_part = jnp.where(row >= col, tiled, flipped)
    imag_part = jnp.where(row < col, tiled, jnp.where(row > col, -flipped, 0.0))
    return jnp.where(above == left, real_part, jnp.where(above, imag_part, -imag_part))


def gram_kernel(spectra_ref, weights_ref, packed_ref, held_ref, near_ref, root_ref, near_sem, sems):
    near = pltpu.make_async_copy(weights_ref, near_ref, near_sem)
    near.start()
    loads = []
    first = 0
    for spot, step in enumerate(LOADS):
        place = pl.ds(first, step)
        loads.append(pltpu.make_async_copy(spectra_ref.at[place], held_ref.at[place], sems.at[spot]))
        loads[-1].start()
        first += step
    near.wait()
    for part in range(near_ref.shape[0]):
        row = jnp.sqrt(near_ref[part : part + 1, :])
        root_ref[part * COLS : (part + 1) * COLS, :] = jnp.broadcast_to(row, (COLS, COLS)).T

    first = 0
    for spot, step in enumerate(LOADS):
        loads[spot].wait()
        for freq in range(first, first + step):
            weighted = (root_ref[...][None] * held_ref[freq].astype(jnp.float32)).astype(jnp.bfloat16)
            rows = weighted.reshape(-1, COLS)
            products = lax.dot_general(
                rows, rows, (((0,), (0,)), ((), ())), preferred_element_type=jnp.float32
            )
            packed_ref[freq] = pack(products)
        first += step


def split(value):
    high = value.astype(jnp.bfloat16)
    low = (value - high.astype(jnp.float32)).astype(jnp.bfloat16)
    return high, low


def left_of(value):
    return jnp.concatenate(split(value), 1)


def right_of(value):
    row = jnp.concatenate(split(value), 1)
    return jnp.concatenate([row, row], 0)


def product(left, right):
    both = jnp.dot(left, right, preferred_element_type=jnp.float32)
    return both[:, :COLS] + both[:, COLS:]


def polar_kernel(parts_ref, packed_ref):
    gram = unpack(jnp.sum(parts_ref[...], 0))
    rows = lax.broadcasted_iota(jnp.int32, (COLS, COLS), 0)
    cols = lax.broadcasted_iota(jnp.int32, (COLS, COLS), 1)
    ident = (rows == cols).astype(jnp.float32)
    trace = jnp.sum(gram * ident)
    inner = gram / trace
    factor = 1.5 * ident - 0.5 * inner
    mapping = factor / jnp.sqrt(trace)
    for sweep in range(NS_STEPS - 1):
        right = right_of(factor)
        half = product(left_of(inner), right)
        inner = product(left_of(half), right)
        if sweep > 0:
            mapping = product(left_of(mapping), right)
        factor = 1.5 * ident - 0.5 * inner
    mapping = product(left_of(mapping), right_of(factor))
    packed = 0.5 * pack(mapping)
    packed_ref[...] = jnp.broadcast_to(packed[None], packed_ref.shape)


def apply_kernel(packed_ref, spectra_ref, shapes_ref, staged_ref, sems):
    saves = []
    first = 0
    for spot, step in enumerate(SAVES):
        for freq in range(first, first + step, 2):
            pair = [unpack(packed_ref[freq + k]).astype(jnp.bfloat16) for k in range(2)]
            blank = jnp.zeros_like(pair[0])
            mapping = jnp.concatenate(
                [jnp.concatenate([pair[0], blank], 1), jnp.concatenate([blank, pair[1]], 1)], 0
            )
            rows = jnp.concatenate([spectra_ref[freq + k].reshape(-1, COLS) for k in range(2)], 1)
            shapes = jnp.dot(rows, mapping, preferred_element_type=jnp.float32).astype(jnp.bfloat16)
            for k in range(2):
                part = shapes[:, k * COLS : (k + 1) * COLS]
                staged_ref[freq + k] = part.reshape(staged_ref.shape[1:])
        place = pl.ds(first, step)
        saves.append(pltpu.make_async_copy(staged_ref.at[place], shapes_ref.at[place], sems.at[spot]))
        saves[-1].start()
        first += step
    for save in saves:
        save.wait()


LOADS = (6, 10)
SAVES = (4, 4, 4, 4)
MIB = 1 << 20


def local(spectra, weights):
    freq_count, var_count, point_count, col_count = spectra.shape
    hbm = pl.BlockSpec(memory_space=pltpu.HBM)
    vmem = pl.BlockSpec(memory_space=pltpu.VMEM)
    packed_shape = (freq_count, HALF // 2, COLS)
    packed, held = pl.pallas_call(
        gram_kernel,
        in_specs=[hbm, hbm],
        out_specs=[vmem, vmem],
        out_shape=[pltpu.VMEM(packed_shape, jnp.float32), pltpu.VMEM(spectra.shape, spectra.dtype)],
        scratch_shapes=[
            pltpu.VMEM((point_count // COLS, COLS), jnp.float32),
            pltpu.VMEM((point_count, COLS), jnp.float32),
            pltpu.SemaphoreType.DMA,
            pltpu.SemaphoreType.DMA((len(LOADS),)),
        ],
        compiler_params=pltpu.CompilerParams(vmem_limit_bytes=8 * MIB),
        name="gram",
    )(
        pltpu.with_memory_space_constraint(spectra, pltpu.HBM),
        pltpu.with_memory_space_constraint(weights.reshape(point_count // COLS, COLS), pltpu.HBM),
    )
    parts = lax.all_to_all(packed, "pts", 0, 0, tiled=True)
    own = pl.pallas_call(
        polar_kernel,
        in_specs=[vmem],
        out_specs=vmem,
        out_shape=pltpu.VMEM(packed_shape, jnp.float32),
        compiler_params=pltpu.CompilerParams(vmem_limit_bytes=8 * MIB),
        name="polar",
    )(pltpu.with_memory_space_constraint(parts, pltpu.VMEM))
    mappings = lax.all_to_all(own, "pts", 0, 0, tiled=True)
    return pl.pallas_call(
        apply_kernel,
        in_specs=[vmem, vmem],
        out_specs=hbm,
        out_shape=jax.ShapeDtypeStruct(spectra.shape, jnp.bfloat16),
        scratch_shapes=[
            pltpu.VMEM(spectra.shape, jnp.bfloat16),
            pltpu.SemaphoreType.DMA((len(SAVES),)),
        ],
        compiler_params=pltpu.CompilerParams(vmem_limit_bytes=16 * MIB),
        name="apply",
    )(pltpu.with_memory_space_constraint(mappings, pltpu.VMEM), held)


def solution(mesh):
    in_specs = (P("freq", None, "pts", None), P("pts"))
    out_specs = P("freq", None, "pts", None)
    return jax.shard_map(local, mesh=mesh, in_specs=in_specs, out_specs=out_specs, check_vma=False)
```

```python
import jax
import jax.numpy as jnp
from jax import lax
from jax.experimental import pallas as pl
from jax.experimental.pallas import tpu as pltpu
from jax.sharding import PartitionSpec as P

NS_STEPS = 10
HALF = 64
COLS = 2 * HALF


def places(rows):
    row = lax.broadcasted_iota(jnp.int32, (rows, COLS), 0)
    col = lax.broadcasted_iota(jnp.int32, (rows, COLS), 1)
    return row % HALF, col % HALF, row < HALF, col < HALF


def pack(square):
    row, col, _, left = places(HALF)
    top, bottom = square[:HALF], square[HALF:]
    lower = row >= col
    chosen = jnp.where(left == lower, top, jnp.where(left, -bottom, bottom))
    upper_rows, lower_rows = chosen[: HALF // 2], chosen[HALF // 2 :]
    left = left[: HALF // 2]
    keep = jnp.where(left, upper_rows, lower_rows)
    move = jnp.where(left, lower_rows, upper_rows)
    return keep + pltpu.roll(move, HALF, 1)


def unpack(packed):
    row, col, above, left = places(COLS)
    turned = pltpu.roll(packed, HALF, 1)
    half_left = left[: HALF // 2]
    upper_rows = jnp.where(half_left, packed, turned)
    lower_rows = jnp.where(half_left, turned, packed)
    tiled = jnp.concatenate([upper_rows, lower_rows, upper_rows, lower_rows], 0)
    flipped = tiled.T
    real_part = jnp.where(row >= col, tiled, flipped)
    imag_part = jnp.where(row < col, tiled, jnp.where(row > col, -flipped, 0.0))
    return jnp.where(above == left, real_part, jnp.where(above, imag_part, -imag_part))


def gram_kernel(spectra_ref, weights_ref, packed_ref, held_ref, near_ref, root_ref, near_sem, sems):
    near = pltpu.make_async_copy(weights_ref, near_ref, near_sem)
    near.start()
    loads = []
    first = 0
    for spot, step in enumerate(LOADS):
        place = pl.ds(first, step)
        loads.append(pltpu.make_async_copy(spectra_ref.at[place], held_ref.at[place], sems.at[spot]))
        loads[-1].start(priority=min(spot, 1))
        first += step
    near.wait()
    for part in range(near_ref.shape[0]):
        row = jnp.sqrt(near_ref[part : part + 1, :])
        root_ref[part * COLS : (part + 1) * COLS, :] = jnp.broadcast_to(row, (COLS, COLS)).T

    first = 0
    for spot, step in enumerate(LOADS):
        loads[spot].wait()
        for freq in range(first, first + step):
            weighted = (root_ref[...][None] * held_ref[freq].astype(jnp.float32)).astype(jnp.bfloat16)
            rows = weighted.reshape(-1, COLS)
            products = lax.dot_general(
                rows, rows, (((0,), (0,)), ((), ())), preferred_element_type=jnp.float32
            )
            packed_ref[freq] = pack(products)
        first += step


def split(value):
    high = value.astype(jnp.bfloat16)
    low = (value - high.astype(jnp.float32)).astype(jnp.bfloat16)
    return high, low


def left_of(value):
    return jnp.concatenate(split(value), 1)


def right_of(value):
    row = jnp.concatenate(split(value), 1)
    return jnp.concatenate([row, row], 0)


def product(left, right):
    both = jnp.dot(left, right, preferred_element_type=jnp.float32)
    return both[:, :COLS] + both[:, COLS:]


def polar_kernel(parts_ref, packed_ref):
    packed = jnp.sum(parts_ref[...], 0)
    gram = unpack(packed)
    row, col, _, left = places(HALF // 2)
    diagonal = jnp.where(left, row, row + HALF // 2) == col
    trace = 2.0 * jnp.sum(jnp.where(diagonal, packed, 0.0), keepdims=True)
    rows = lax.broadcasted_iota(jnp.int32, (COLS, COLS), 0)
    cols = lax.broadcasted_iota(jnp.int32, (COLS, COLS), 1)
    ident = (rows == cols).astype(jnp.float32)
    inner = gram * (1.0 / trace)
    factor = 1.5 * ident - 0.5 * inner
    mapping = factor * (1.0 / jnp.sqrt(trace))
    for sweep in range(NS_STEPS - 1):
        right = right_of(factor)
        half = product(left_of(inner), right)
        inner = product(left_of(half), right)
        if sweep > 0:
            mapping = product(left_of(mapping), right)
        factor = 1.5 * ident - 0.5 * inner
    mapping = product(left_of(mapping), right_of(factor))
    packed = 0.5 * pack(mapping)
    packed_ref[...] = jnp.broadcast_to(packed[None], packed_ref.shape)


def apply_kernel(packed_ref, spectra_ref, shapes_ref, staged_ref, sems):
    saves = []
    first = 0
    for spot, step in enumerate(SAVES):
        for freq in range(first, first + step, 2):
            pair = [unpack(packed_ref[freq + k]).astype(jnp.bfloat16) for k in range(2)]
            blank = jnp.zeros_like(pair[0])
            mapping = jnp.concatenate(
                [jnp.concatenate([pair[0], blank], 1), jnp.concatenate([blank, pair[1]], 1)], 0
            )
            rows = jnp.concatenate([spectra_ref[freq + k].reshape(-1, COLS) for k in range(2)], 1)
            shapes = jnp.dot(rows, mapping, preferred_element_type=jnp.float32).astype(jnp.bfloat16)
            for k in range(2):
                part = shapes[:, k * COLS : (k + 1) * COLS]
                staged_ref[freq + k] = part.reshape(staged_ref.shape[1:])
        place = pl.ds(first, step)
        saves.append(pltpu.make_async_copy(staged_ref.at[place], shapes_ref.at[place], sems.at[spot]))
        saves[-1].start()
        first += step
    for save in saves:
        save.wait()


LOADS = (4, 6, 6)
SAVES = (4, 4, 4, 4)
MIB = 1 << 20


def local(spectra, weights):
    freq_count, var_count, point_count, col_count = spectra.shape
    hbm = pl.BlockSpec(memory_space=pltpu.HBM)
    vmem = pl.BlockSpec(memory_space=pltpu.VMEM)
    packed_shape = (freq_count, HALF // 2, COLS)
    packed, held = pl.pallas_call(
        gram_kernel,
        in_specs=[hbm, hbm],
        out_specs=[vmem, vmem],
        out_shape=[pltpu.VMEM(packed_shape, jnp.float32), pltpu.VMEM(spectra.shape, spectra.dtype)],
        scratch_shapes=[
            pltpu.VMEM((point_count // COLS, COLS), jnp.float32),
            pltpu.VMEM((point_count, COLS), jnp.float32),
            pltpu.SemaphoreType.DMA,
            pltpu.SemaphoreType.DMA((len(LOADS),)),
        ],
        compiler_params=pltpu.CompilerParams(vmem_limit_bytes=8 * MIB),
        name="gram",
    )(
        pltpu.with_memory_space_constraint(spectra, pltpu.HBM),
        pltpu.with_memory_space_constraint(weights.reshape(point_count // COLS, COLS), pltpu.HBM),
    )
    parts = lax.all_to_all(packed, "pts", 0, 0, tiled=True)
    own = pl.pallas_call(
        polar_kernel,
        in_specs=[vmem],
        out_specs=vmem,
        out_shape=pltpu.VMEM(packed_shape, jnp.float32),
        compiler_params=pltpu.CompilerParams(vmem_limit_bytes=8 * MIB),
        name="polar",
    )(pltpu.with_memory_space_constraint(parts, pltpu.VMEM))
    mappings = lax.all_to_all(own, "pts", 0, 0, tiled=True)
    return pl.pallas_call(
        apply_kernel,
        in_specs=[vmem, vmem],
        out_specs=hbm,
        out_shape=jax.ShapeDtypeStruct(spectra.shape, jnp.bfloat16),
        scratch_shapes=[
            pltpu.VMEM(spectra.shape, jnp.bfloat16),
            pltpu.SemaphoreType.DMA((len(SAVES),)),
        ],
        compiler_params=pltpu.CompilerParams(vmem_limit_bytes=16 * MIB),
        name="apply",
    )(pltpu.with_memory_space_constraint(mappings, pltpu.VMEM), held)


def solution(mesh):
    in_specs = (P("freq", None, "pts", None), P("pts"))
    out_specs = P("freq", None, "pts", None)
    return jax.shard_map(local, mesh=mesh, in_specs=in_specs, out_specs=out_specs, check_vma=False)
```

```python
import jax
import jax.numpy as jnp
from jax import lax
from jax.experimental import pallas as pl
from jax.experimental.pallas import tpu as pltpu
from jax.sharding import PartitionSpec as P

NS_STEPS = 10
HALF = 64
COLS = 2 * HALF


def places(rows):
    row = lax.broadcasted_iota(jnp.int32, (rows, COLS), 0)
    col = lax.broadcasted_iota(jnp.int32, (rows, COLS), 1)
    return row % HALF, col % HALF, row < HALF, col < HALF


def pack(square):
    row, col, _, left = places(HALF)
    top, bottom = square[:HALF], square[HALF:]
    lower = row >= col
    chosen = jnp.where(left == lower, top, jnp.where(left, -bottom, bottom))
    upper_rows, lower_rows = chosen[: HALF // 2], chosen[HALF // 2 :]
    left = left[: HALF // 2]
    keep = jnp.where(left, upper_rows, lower_rows)
    move = jnp.where(left, lower_rows, upper_rows)
    return keep + pltpu.roll(move, HALF, 1)


def unpack(packed):
    row, col, above, left = places(COLS)
    turned = pltpu.roll(packed, HALF, 1)
    half_left = left[: HALF // 2]
    upper_rows = jnp.where(half_left, packed, turned)
    lower_rows = jnp.where(half_left, turned, packed)
    tiled = jnp.concatenate([upper_rows, lower_rows, upper_rows, lower_rows], 0)
    flipped = tiled.T
    real_part = jnp.where(row >= col, tiled, flipped)
    imag_part = jnp.where(row < col, tiled, jnp.where(row > col, -flipped, 0.0))
    return jnp.where(above == left, real_part, jnp.where(above, imag_part, -imag_part))


def gram_kernel(spectra_ref, weights_ref, packed_ref, held_ref, near_ref, root_ref, near_sem, sems):
    near = pltpu.make_async_copy(weights_ref, near_ref, near_sem)
    near.start()
    loads = []
    first = 0
    for spot, step in enumerate(LOADS):
        place = pl.ds(first, step)
        loads.append(pltpu.make_async_copy(spectra_ref.at[place], held_ref.at[place], sems.at[spot]))
        loads[-1].start(priority=min(spot, 1))
        first += step
    near.wait()
    for part in range(near_ref.shape[0]):
        row = jnp.sqrt(near_ref[part : part + 1, :])
        root_ref[part * COLS : (part + 1) * COLS, :] = jnp.broadcast_to(row, (COLS, COLS)).T

    first = 0
    for spot, step in enumerate(LOADS):
        loads[spot].wait()
        for freq in range(first, first + step):
            weighted = (root_ref[...][None] * held_ref[freq].astype(jnp.float32)).astype(jnp.bfloat16)
            rows = weighted.reshape(-1, COLS)
            products = lax.dot_general(
                rows, rows, (((0,), (0,)), ((), ())), preferred_element_type=jnp.float32
            )
            packed_ref[freq] = pack(products)
        first += step


def split(value):
    high = value.astype(jnp.bfloat16)
    low = (value - high.astype(jnp.float32)).astype(jnp.bfloat16)
    return high, low


def left_of(value):
    return jnp.concatenate(split(value), 1)


def right_of(value):
    row = jnp.concatenate(split(value), 1)
    return jnp.concatenate([row, row], 0)


def product(left, right):
    both = jnp.dot(left, right, preferred_element_type=jnp.float32)
    return both[:, :COLS] + both[:, COLS:]


def polar_kernel(parts_ref, packed_ref):
    packed = jnp.sum(parts_ref[...], 0)
    gram = unpack(packed)
    row, col, _, left = places(HALF // 2)
    diagonal = jnp.where(left, row, row + HALF // 2) == col
    trace = 2.0 * jnp.sum(jnp.where(diagonal, packed, 0.0), keepdims=True)
    rows = lax.broadcasted_iota(jnp.int32, (COLS, COLS), 0)
    cols = lax.broadcasted_iota(jnp.int32, (COLS, COLS), 1)
    ident = (rows == cols).astype(jnp.float32)
    inner = gram * (1.0 / trace)
    factor = 1.5 * ident - 0.5 * inner
    mapping = factor[:HALF] * (1.0 / jnp.sqrt(trace))
    for sweep in range(NS_STEPS - 1):
        right = right_of(factor)
        half = product(left_of(inner), right)
        inner = product(left_of(half), right)
        if sweep > 0:
            mapping = product(left_of(mapping), right)
        factor = 1.5 * ident - 0.5 * inner
    mapping = product(left_of(mapping), right_of(factor))
    packed = pack(jnp.concatenate([mapping, jnp.zeros_like(mapping)], 0))
    for spot in range(packed_ref.shape[0]):
        packed_ref[spot] = packed


def apply_kernel(packed_ref, spectra_ref, shapes_ref, staged_ref, sems):
    saves = []
    first = 0
    for spot, step in enumerate(SAVES):
        for freq in range(first, first + step, 2):
            pair = [unpack(packed_ref[freq + k]).astype(jnp.bfloat16) for k in range(2)]
            blank = jnp.zeros_like(pair[0])
            mapping = jnp.concatenate(
                [jnp.concatenate([pair[0], blank], 1), jnp.concatenate([blank, pair[1]], 1)], 0
            )
            rows = jnp.concatenate([spectra_ref[freq + k].reshape(-1, COLS) for k in range(2)], 1)
            shapes = jnp.dot(rows, mapping, preferred_element_type=jnp.float32).astype(jnp.bfloat16)
            for k in range(2):
                part = shapes[:, k * COLS : (k + 1) * COLS]
                staged_ref[freq + k] = part.reshape(staged_ref.shape[1:])
        place = pl.ds(first, step)
        saves.append(pltpu.make_async_copy(staged_ref.at[place], shapes_ref.at[place], sems.at[spot]))
        saves[-1].start()
        first += step
    for save in saves:
        save.wait()


LOADS = (4, 6, 6)
SAVES = (4, 4, 4, 4)
MIB = 1 << 20


def local(spectra, weights):
    freq_count, var_count, point_count, col_count = spectra.shape
    hbm = pl.BlockSpec(memory_space=pltpu.HBM)
    vmem = pl.BlockSpec(memory_space=pltpu.VMEM)
    packed_shape = (freq_count, HALF // 2, COLS)
    packed, held = pl.pallas_call(
        gram_kernel,
        in_specs=[hbm, hbm],
        out_specs=[vmem, vmem],
        out_shape=[pltpu.VMEM(packed_shape, jnp.float32), pltpu.VMEM(spectra.shape, spectra.dtype)],
        scratch_shapes=[
            pltpu.VMEM((point_count // COLS, COLS), jnp.float32),
            pltpu.VMEM((point_count, COLS), jnp.float32),
            pltpu.SemaphoreType.DMA,
            pltpu.SemaphoreType.DMA((len(LOADS),)),
        ],
        compiler_params=pltpu.CompilerParams(vmem_limit_bytes=8 * MIB),
        name="gram",
    )(
        pltpu.with_memory_space_constraint(spectra, pltpu.HBM),
        pltpu.with_memory_space_constraint(weights.reshape(point_count // COLS, COLS), pltpu.HBM),
    )
    parts = lax.all_to_all(packed, "pts", 0, 0, tiled=True)
    own = pl.pallas_call(
        polar_kernel,
        in_specs=[vmem],
        out_specs=vmem,
        out_shape=pltpu.VMEM(packed_shape, jnp.float32),
        compiler_params=pltpu.CompilerParams(vmem_limit_bytes=8 * MIB),
        name="polar",
    )(pltpu.with_memory_space_constraint(parts, pltpu.VMEM))
    mappings = lax.all_to_all(own, "pts", 0, 0, tiled=True)
    return pl.pallas_call(
        apply_kernel,
        in_specs=[vmem, vmem],
        out_specs=hbm,
        out_shape=jax.ShapeDtypeStruct(spectra.shape, jnp.bfloat16),
        scratch_shapes=[
            pltpu.VMEM(spectra.shape, jnp.bfloat16),
            pltpu.SemaphoreType.DMA((len(SAVES),)),
        ],
        compiler_params=pltpu.CompilerParams(vmem_limit_bytes=16 * MIB),
        name="apply",
    )(pltpu.with_memory_space_constraint(mappings, pltpu.VMEM), held)


def solution(mesh):
    in_specs = (P("freq", None, "pts", None), P("pts"))
    out_specs = P("freq", None, "pts", None)
    return jax.shard_map(local, mesh=mesh, in_specs=in_specs, out_specs=out_specs, check_vma=False)
```

```python
import jax
import jax.numpy as jnp
from jax import lax
from jax.experimental import pallas as pl
from jax.experimental.pallas import tpu as pltpu
from jax.sharding import PartitionSpec as P

NS_STEPS = 10
HALF = 64
COLS = 2 * HALF


def places(rows):
    row = lax.broadcasted_iota(jnp.int32, (rows, COLS), 0)
    col = lax.broadcasted_iota(jnp.int32, (rows, COLS), 1)
    return row % HALF, col % HALF, row < HALF, col < HALF


def pack(square):
    row, col, _, left = places(HALF)
    top, bottom = square[:HALF], square[HALF:]
    lower = row >= col
    chosen = jnp.where(left == lower, top, jnp.where(left, -bottom, bottom))
    upper_rows, lower_rows = chosen[: HALF // 2], chosen[HALF // 2 :]
    left = left[: HALF // 2]
    keep = jnp.where(left, upper_rows, lower_rows)
    move = jnp.where(left, lower_rows, upper_rows)
    return keep + pltpu.roll(move, HALF, 1)


def unpack(packed, dtype):
    row, col, above, left = places(COLS)
    turned = pltpu.roll(packed, HALF, 1)
    half_left = left[: HALF // 2]
    upper_rows = jnp.where(half_left, packed, turned)
    lower_rows = jnp.where(half_left, turned, packed)
    tiled = jnp.concatenate([upper_rows, lower_rows, upper_rows, lower_rows], 0).astype(dtype)
    flipped = tiled.T
    real_part = jnp.where(row >= col, tiled, flipped)
    imag_part = jnp.where(row < col, tiled, jnp.where(row > col, -flipped, jnp.zeros_like(tiled)))
    return jnp.where(above == left, real_part, jnp.where(above, imag_part, -imag_part))


def gram_kernel(spectra_ref, weights_ref, packed_ref, held_ref, near_ref, root_ref, near_sem, sems):
    near = pltpu.make_async_copy(weights_ref, near_ref, near_sem)
    near.start()
    loads = []
    first = 0
    for spot, step in enumerate(LOADS):
        place = pl.ds(first, step)
        loads.append(pltpu.make_async_copy(spectra_ref.at[place], held_ref.at[place], sems.at[spot]))
        loads[-1].start(priority=min(spot, 1))
        first += step
    near.wait()
    for part in range(near_ref.shape[0]):
        row = jnp.sqrt(near_ref[part : part + 1, :])
        root_ref[part * COLS : (part + 1) * COLS, :] = jnp.broadcast_to(row, (COLS, COLS)).T

    first = 0
    for spot, step in enumerate(LOADS):
        loads[spot].wait()
        for freq in range(first, first + step):
            weighted = (root_ref[...][None] * held_ref[freq].astype(jnp.float32)).astype(jnp.bfloat16)
            rows = weighted.reshape(-1, COLS)
            products = lax.dot_general(
                rows, rows, (((0,), (0,)), ((), ())), preferred_element_type=jnp.float32
            )
            packed_ref[freq] = pack(products)
        first += step


def split(value):
    high = value.astype(jnp.bfloat16)
    low = (value - high.astype(jnp.float32)).astype(jnp.bfloat16)
    return high, low


def left_of(value):
    return jnp.concatenate(split(value), 1)


def right_of(value):
    row = jnp.concatenate(split(value), 1)
    return jnp.concatenate([row, row], 0)


def product(left, right):
    both = jnp.dot(left, right, preferred_element_type=jnp.float32)
    return both[:, :COLS] + both[:, COLS:]


def polar_kernel(parts_ref, packed_ref):
    packed = jnp.sum(parts_ref[...], 0)
    gram = unpack(packed, jnp.float32)
    row, col, _, left = places(HALF // 2)
    diagonal = jnp.where(left, row, row + HALF // 2) == col
    trace = 2.0 * jnp.sum(jnp.where(diagonal, packed, 0.0), keepdims=True)
    rows = lax.broadcasted_iota(jnp.int32, (COLS, COLS), 0)
    cols = lax.broadcasted_iota(jnp.int32, (COLS, COLS), 1)
    ident = (rows == cols).astype(jnp.float32)
    inner = gram * (1.0 / trace)
    factor = 1.5 * ident - 0.5 * inner
    mapping = factor[:HALF] * (1.0 / jnp.sqrt(trace))
    for sweep in range(NS_STEPS - 1):
        right = right_of(factor)
        half = product(left_of(inner), right)
        inner = product(left_of(half), right)
        if sweep > 0:
            mapping = product(left_of(mapping), right)
        factor = 1.5 * ident - 0.5 * inner
    mapping = product(left_of(mapping), right_of(factor))
    packed = pack(jnp.concatenate([mapping, jnp.zeros_like(mapping)], 0))
    for spot in range(packed_ref.shape[0]):
        packed_ref[spot] = packed


def apply_kernel(packed_ref, spectra_ref, shapes_ref, staged_ref, sems):
    saves = []
    first = 0
    for spot, step in enumerate(SAVES):
        for freq in range(first, first + step, 2):
            pair = [unpack(packed_ref[freq + k], jnp.bfloat16) for k in range(2)]
            blank = jnp.zeros_like(pair[0])
            mapping = jnp.concatenate(
                [jnp.concatenate([pair[0], blank], 1), jnp.concatenate([blank, pair[1]], 1)], 0
            )
            rows = jnp.concatenate([spectra_ref[freq + k].reshape(-1, COLS) for k in range(2)], 1)
            shapes = jnp.dot(rows, mapping, preferred_element_type=jnp.float32).astype(jnp.bfloat16)
            for k in range(2):
                part = shapes[:, k * COLS : (k + 1) * COLS]
                staged_ref[freq + k] = part.reshape(staged_ref.shape[1:])
        place = pl.ds(first, step)
        saves.append(pltpu.make_async_copy(staged_ref.at[place], shapes_ref.at[place], sems.at[spot]))
        saves[-1].start()
        first += step
    for save in saves:
        save.wait()


LOADS = (4, 6, 6)
SAVES = (4, 4, 4, 4)
MIB = 1 << 20


def local(spectra, weights):
    freq_count, var_count, point_count, col_count = spectra.shape
    hbm = pl.BlockSpec(memory_space=pltpu.HBM)
    vmem = pl.BlockSpec(memory_space=pltpu.VMEM)
    packed_shape = (freq_count, HALF // 2, COLS)
    packed, held = pl.pallas_call(
        gram_kernel,
        in_specs=[hbm, hbm],
        out_specs=[vmem, vmem],
        out_shape=[pltpu.VMEM(packed_shape, jnp.float32), pltpu.VMEM(spectra.shape, spectra.dtype)],
        scratch_shapes=[
            pltpu.VMEM((point_count // COLS, COLS), jnp.float32),
            pltpu.VMEM((point_count, COLS), jnp.float32),
            pltpu.SemaphoreType.DMA,
            pltpu.SemaphoreType.DMA((len(LOADS),)),
        ],
        compiler_params=pltpu.CompilerParams(vmem_limit_bytes=8 * MIB),
        name="gram",
    )(
        pltpu.with_memory_space_constraint(spectra, pltpu.HBM),
        pltpu.with_memory_space_constraint(weights.reshape(point_count // COLS, COLS), pltpu.HBM),
    )
    parts = lax.all_to_all(packed, "pts", 0, 0, tiled=True)
    own = pl.pallas_call(
        polar_kernel,
        in_specs=[vmem],
        out_specs=vmem,
        out_shape=pltpu.VMEM(packed_shape, jnp.float32),
        compiler_params=pltpu.CompilerParams(vmem_limit_bytes=8 * MIB),
        name="polar",
    )(pltpu.with_memory_space_constraint(parts, pltpu.VMEM))
    mappings = lax.all_to_all(own, "pts", 0, 0, tiled=True)
    return pl.pallas_call(
        apply_kernel,
        in_specs=[vmem, vmem],
        out_specs=hbm,
        out_shape=jax.ShapeDtypeStruct(spectra.shape, jnp.bfloat16),
        scratch_shapes=[
            pltpu.VMEM(spectra.shape, jnp.bfloat16),
            pltpu.SemaphoreType.DMA((len(SAVES),)),
        ],
        compiler_params=pltpu.CompilerParams(vmem_limit_bytes=16 * MIB),
        name="apply",
    )(pltpu.with_memory_space_constraint(mappings, pltpu.VMEM), held)


def solution(mesh):
    in_specs = (P("freq", None, "pts", None), P("pts"))
    out_specs = P("freq", None, "pts", None)
    return jax.shard_map(local, mesh=mesh, in_specs=in_specs, out_specs=out_specs, check_vma=False)
```

```python
import jax
import jax.numpy as jnp
from jax import lax
from jax.experimental import pallas as pl
from jax.experimental.pallas import tpu as pltpu
from jax.sharding import PartitionSpec as P

NS_STEPS = 10
HALF = 64
COLS = 2 * HALF


def places(rows):
    row = lax.broadcasted_iota(jnp.int32, (rows, COLS), 0)
    col = lax.broadcasted_iota(jnp.int32, (rows, COLS), 1)
    return row % HALF, col % HALF, row < HALF, col < HALF


def pack(square):
    row, col, _, left = places(HALF)
    top, bottom = square[:HALF], square[HALF:]
    lower = row >= col
    chosen = jnp.where(left == lower, top, jnp.where(left, -bottom, bottom))
    upper_rows, lower_rows = chosen[: HALF // 2], chosen[HALF // 2 :]
    left = left[: HALF // 2]
    keep = jnp.where(left, upper_rows, lower_rows)
    move = jnp.where(left, lower_rows, upper_rows)
    return keep + pltpu.roll(move, HALF, 1)


def unpack(packed, dtype):
    row, col, above, left = places(COLS)
    turned = pltpu.roll(packed, HALF, 1)
    half_left = left[: HALF // 2]
    upper_rows = jnp.where(half_left, packed, turned)
    lower_rows = jnp.where(half_left, turned, packed)
    tiled = jnp.concatenate([upper_rows, lower_rows, upper_rows, lower_rows], 0).astype(dtype)
    flipped = tiled.T
    real_part = jnp.where(row >= col, tiled, flipped)
    imag_part = jnp.where(row < col, tiled, jnp.where(row > col, -flipped, jnp.zeros_like(tiled)))
    return jnp.where(above == left, real_part, jnp.where(above, imag_part, -imag_part))


def gram_kernel(spectra_ref, weights_ref, packed_ref, held_ref, near_ref, root_ref, near_sem, sems):
    near = pltpu.make_async_copy(weights_ref, near_ref, near_sem)
    near.start()
    loads = []
    first = 0
    for spot, step in enumerate(LOADS):
        place = pl.ds(first, step)
        loads.append(pltpu.make_async_copy(spectra_ref.at[place], held_ref.at[place], sems.at[spot]))
        loads[-1].start(priority=min(spot, 1))
        first += step
    near.wait()
    for part in range(near_ref.shape[0]):
        row = jnp.sqrt(near_ref[part : part + 1, :])
        root_ref[part * COLS : (part + 1) * COLS, :] = jnp.broadcast_to(row, (COLS, COLS)).T

    first = 0
    for spot, step in enumerate(LOADS):
        loads[spot].wait()
        for freq in range(first, first + step):
            weighted = (root_ref[...][None] * held_ref[freq].astype(jnp.float32)).astype(jnp.bfloat16)
            rows = weighted.reshape(-1, COLS)
            products = lax.dot_general(
                rows, rows, (((0,), (0,)), ((), ())), preferred_element_type=jnp.float32
            )
            packed_ref[freq] = pack(products)
        first += step


def split(value):
    high = value.astype(jnp.bfloat16)
    low = (value - high.astype(jnp.float32)).astype(jnp.bfloat16)
    return high, low


def left_of(value):
    return jnp.concatenate(split(value), 1)


def right_of(value):
    row = jnp.concatenate(split(value), 1)
    return jnp.concatenate([row, row], 0)


def product(left, right):
    both = jnp.dot(left, right, preferred_element_type=jnp.float32)
    return both[:, :COLS] + both[:, COLS:]


def polar_kernel(parts_ref, packed_ref):
    terms = [parts_ref[spot] for spot in range(parts_ref.shape[0])]
    while len(terms) > 1:
        terms = [terms[spot] + terms[spot + 1] for spot in range(0, len(terms), 2)]
    packed = terms[0]
    gram = unpack(packed, jnp.float32)
    row, col, _, left = places(HALF // 2)
    diagonal = jnp.where(left, row, row + HALF // 2) == col
    trace = 2.0 * jnp.sum(jnp.where(diagonal, packed, 0.0), keepdims=True)
    rows = lax.broadcasted_iota(jnp.int32, (COLS, COLS), 0)
    cols = lax.broadcasted_iota(jnp.int32, (COLS, COLS), 1)
    ident = (rows == cols).astype(jnp.float32)
    inner = gram * (1.0 / trace)
    factor = 1.5 * ident - 0.5 * inner
    mapping = factor[:HALF] * (1.0 / jnp.sqrt(trace))
    for sweep in range(NS_STEPS - 1):
        right = right_of(factor)
        half = product(left_of(inner), right)
        inner = product(left_of(half), right)
        if sweep > 0:
            mapping = product(left_of(mapping), right)
        factor = 1.5 * ident - 0.5 * inner
    mapping = product(left_of(mapping), right_of(factor))
    packed = pack(jnp.concatenate([mapping, jnp.zeros_like(mapping)], 0))
    for spot in range(packed_ref.shape[0]):
        packed_ref[spot] = packed


def apply_kernel(packed_ref, spectra_ref, shapes_ref, staged_ref, sems):
    saves = []
    first = 0
    for spot, step in enumerate(SAVES):
        for freq in range(first, first + step, 2):
            pair = [unpack(packed_ref[freq + k], jnp.bfloat16) for k in range(2)]
            blank = jnp.zeros_like(pair[0])
            mapping = jnp.concatenate(
                [jnp.concatenate([pair[0], blank], 1), jnp.concatenate([blank, pair[1]], 1)], 0
            )
            rows = jnp.concatenate([spectra_ref[freq + k].reshape(-1, COLS) for k in range(2)], 1)
            shapes = jnp.dot(rows, mapping, preferred_element_type=jnp.float32).astype(jnp.bfloat16)
            for k in range(2):
                part = shapes[:, k * COLS : (k + 1) * COLS]
                staged_ref[freq + k] = part.reshape(staged_ref.shape[1:])
        place = pl.ds(first, step)
        saves.append(pltpu.make_async_copy(staged_ref.at[place], shapes_ref.at[place], sems.at[spot]))
        saves[-1].start()
        first += step
    for save in saves:
        save.wait()


LOADS = (4, 6, 6)
SAVES = (4, 4, 4, 4)
MIB = 1 << 20


def local(spectra, weights):
    freq_count, var_count, point_count, col_count = spectra.shape
    hbm = pl.BlockSpec(memory_space=pltpu.HBM)
    vmem = pl.BlockSpec(memory_space=pltpu.VMEM)
    packed_shape = (freq_count, HALF // 2, COLS)
    packed, held = pl.pallas_call(
        gram_kernel,
        in_specs=[hbm, hbm],
        out_specs=[vmem, vmem],
        out_shape=[pltpu.VMEM(packed_shape, jnp.float32), pltpu.VMEM(spectra.shape, spectra.dtype)],
        scratch_shapes=[
            pltpu.VMEM((point_count // COLS, COLS), jnp.float32),
            pltpu.VMEM((point_count, COLS), jnp.float32),
            pltpu.SemaphoreType.DMA,
            pltpu.SemaphoreType.DMA((len(LOADS),)),
        ],
        compiler_params=pltpu.CompilerParams(vmem_limit_bytes=8 * MIB),
        name="gram",
    )(
        pltpu.with_memory_space_constraint(spectra, pltpu.HBM),
        pltpu.with_memory_space_constraint(weights.reshape(point_count // COLS, COLS), pltpu.HBM),
    )
    parts = lax.all_to_all(packed, "pts", 0, 0, tiled=True)
    own = pl.pallas_call(
        polar_kernel,
        in_specs=[vmem],
        out_specs=vmem,
        out_shape=pltpu.VMEM(packed_shape, jnp.float32),
        compiler_params=pltpu.CompilerParams(vmem_limit_bytes=8 * MIB),
        name="polar",
    )(pltpu.with_memory_space_constraint(parts, pltpu.VMEM))
    mappings = lax.all_to_all(own, "pts", 0, 0, tiled=True)
    return pl.pallas_call(
        apply_kernel,
        in_specs=[vmem, vmem],
        out_specs=hbm,
        out_shape=jax.ShapeDtypeStruct(spectra.shape, jnp.bfloat16),
        scratch_shapes=[
            pltpu.VMEM(spectra.shape, jnp.bfloat16),
            pltpu.SemaphoreType.DMA((len(SAVES),)),
        ],
        compiler_params=pltpu.CompilerParams(vmem_limit_bytes=16 * MIB),
        name="apply",
    )(pltpu.with_memory_space_constraint(mappings, pltpu.VMEM), held)


def solution(mesh):
    in_specs = (P("freq", None, "pts", None), P("pts"))
    out_specs = P("freq", None, "pts", None)
    return jax.shard_map(local, mesh=mesh, in_specs=in_specs, out_specs=out_specs, check_vma=False)
```
